32 devices in a mesh: gz: 2 (over y), xy: 16 (over z, x, core).
Axes of the slice: x: 2, y: 2, z: 4, core: 2. Of those that a mesh axis runs over, the one named last changes fastest.
Arguments:
- stack: bfloat16 [32, 256, 2048], P('gz', 'xy'), may hold values from -8 to 8
Outputs:
- joined: float32 [256, 2048], P('xy', 'gz')
- pooled: float32 [128, 1024], P('xy', 'gz')
The draws below stay inside these ranges and needn't reach their ends.
All inputs are finite; a program needn't handle non-finite values.
Results may differ from the reference program's by a relative error of at most 0.0003.
Values may be sent and summed in bfloat16 or wider, within the bound.
A program may use at most 128 MiB of HBM per device.

```python
import jax
import jax.numpy as jnp
from jax import lax

PLANES = 32
HEIGHT = 256
WIDTH = 2048


def draw_stack(key, part):
    key_amp, key_base = jax.random.split(key, 2)
    amp_log = jax.random.uniform(key_amp, (PLANES, HEIGHT // 8, WIDTH // 8), jnp.float32, jnp.log(0.04), jnp.log(0.4))
    amplitude = jnp.repeat(jnp.repeat(jnp.exp(amp_log), 8, axis=1), 8, axis=2)
    texture = jax.random.normal(key_base, (PLANES, HEIGHT, WIDTH), jnp.float32)
    stack = jnp.clip(texture * amplitude, -8.0, 8.0)
    return stack.astype(jnp.bfloat16)


def setup_inputs(seed: int = 0) -> dict:
    key_of = jax.random.split(jax.random.key(seed), 2)
    return {
        "stack": draw_stack(jax.random.fold_in(key_of[1], 71), 0),
    }


sharpness = 0.016
laplace_taps = ((0, 0, 16.0), (1, 0, -2.0), (-1, 0, -2.0), (0, 1, -2.0), (0, -1, -2.0), (1, 1, -1.0), (1, -1, -1.0), (-1, 1, -1.0), (-1, -1, -1.0), (2, 0, -1.0), (-2, 0, -1.0), (0, 2, -1.0), (0, -2, -1.0))


def plane_score(plane):
    height, breadth = plane.shape
    padded = jnp.pad(plane.astype(jnp.float32), 2)
    laplace_out = jnp.zeros((height, breadth), jnp.float32)
    for row_step, col_step, weight in laplace_taps:
        laplace_out = laplace_out + weight * padded[2 + row_step:2 + row_step + height, 2 + col_step:2 + col_step + breadth]
    energy = laplace_out * laplace_out
    padded_energy = jnp.pad(energy, 2)
    row_total = jnp.zeros((height, breadth + 4), jnp.float32)
    for shift_amount in range(-2, 3):
        row_total = row_total + padded_energy[2 + shift_amount:2 + shift_amount + height, :]
    box_total = jnp.zeros((height, breadth), jnp.float32)
    for shift_amount in range(-2, 3):
        box_total = box_total + row_total[:, 2 + shift_amount:2 + shift_amount + breadth]
    return box_total * sharpness


def reference(stack):
    height, breadth = stack.shape[1], stack.shape[2]

    def advance(carry, plane):
        running_max, weighted_sum, weight_sum = carry
        score = plane_score(plane)
        new_max = jnp.maximum(running_max, score)
        old_scale = jnp.exp(running_max - new_max)
        new_scale = jnp.exp(score - new_max)
        weighted_sum = weighted_sum * old_scale + new_scale * plane.astype(jnp.float32)
        weight_sum = weight_sum * old_scale + new_scale
        return (new_max, weighted_sum, weight_sum), None

    start = (jnp.full((height, breadth), -1e30, jnp.float32), jnp.zeros((height, breadth), jnp.float32), jnp.zeros((height, breadth), jnp.float32))
    (final_max, weighted_sum, weight_sum), unused = lax.scan(advance, start, stack)
    joined = weighted_sum / weight_sum
    pooled = joined.reshape(height // 2, 2, breadth // 2, 2).mean(axis=(1, 3))
    return joined, pooled
```

```python
import functools

import jax
import jax.numpy as jnp
from jax import lax
from jax.experimental import pallas as pl
from jax.experimental.pallas import tpu as pltpu
from jax.sharding import PartitionSpec as P

sharpness = 0.016
LANES = 128
HALO = 4
MESH = pl.DeviceIdType.MESH


def cols(tile, count):
    return pl.ds(pl.multiple_of(tile * LANES, LANES), count * LANES)


def from_left(tiles, step, lane):
    rolled = [pltpu.roll(t, step, 1) for t in tiles]
    return [jnp.where(lane < step, rolled[i], rolled[i + 1]) for i in range(len(tiles) - 1)]


def from_right(tiles, step, lane):
    rolled = [pltpu.roll(t, LANES - step, 1) for t in tiles]
    return [
        jnp.where(lane < LANES - step, rolled[i], rolled[i + 1]) for i in range(len(tiles) - 1)
    ]


def kernel(
    geom, x_hbm, joined_ref, pooled_ref,
    xin, top_in, bot_in, top_out, bot_out, xs, es, vs, ss, own, outbox, inbox, jt,
    load_sem, halo_send, halo_recv, gz_send, gz_recv,
):
    planes, rows, tiles, gz_count, xy_count, own_tiles, groups = geom
    gz = lax.axis_index("gz")
    xy = lax.axis_index("xy")
    has_up = xy > 0
    has_down = xy < xy_count - 1

    if gz_count == 2:
        near = own_tiles + 2
        parts = [
            (jnp.where(gz == 0, tiles - near, 0), near),
            (jnp.where(gz == 0, 0, near), tiles - near),
        ]
    else:
        parts = [(0, tiles)]

    def load(part):
        start, size = parts[part]
        return pltpu.make_async_copy(
            x_hbm.at[:, :, cols(start, size)], xin.at[:, :, cols(start + 1, size)], load_sem.at[part]
        )

    for part in range(len(parts)):
        load(part).start()

    barrier = pltpu.get_barrier_semaphore()

    @pl.when(has_up)
    def _():
        pl.semaphore_signal(barrier, inc=1, device_id={"xy": xy - 1}, device_id_type=MESH)

    @pl.when(has_down)
    def _():
        pl.semaphore_signal(barrier, inc=1, device_id={"xy": xy + 1}, device_id_type=MESH)

    for step in range(gz_count - 1):
        peer = lax.rem(gz + 1 + step, gz_count)
        pl.semaphore_signal(barrier, inc=1, device_id={"gz": peer}, device_id_type=MESH)

    def to_up(part):
        start, size = parts[part]
        return pltpu.make_async_remote_copy(
            src_ref=top_out.at[:, :, cols(start, size)],
            dst_ref=bot_in.at[:, :, cols(start + 1, size)],
            send_sem=halo_send.at[0, part], recv_sem=halo_recv.at[0, part],
            device_id={"xy": xy - 1}, device_id_type=MESH,
        )

    def to_down(part):
        start, size = parts[part]
        return pltpu.make_async_remote_copy(
            src_ref=bot_out.at[:, :, cols(start, size)],
            dst_ref=top_in.at[:, :, cols(start + 1, size)],
            send_sem=halo_send.at[1, part], recv_sem=halo_recv.at[1, part],
            device_id={"xy": xy + 1}, device_id_type=MESH,
        )

    for tile in (0, tiles + 1):
        side = pl.ds(tile * LANES, LANES)
        xin[:, :, side] = jnp.zeros((planes, rows, LANES), xin.dtype)
        top_in[:, :, side] = jnp.zeros((planes, HALO, LANES), xin.dtype)
        bot_in[:, :, side] = jnp.zeros((planes, HALO, LANES), xin.dtype)
        vs[:, tile] = jnp.zeros((planes, rows, LANES), jnp.float32)
    xs[:, rows + 12 : rows + 16, :] = jnp.zeros((xs.shape[0], 4, LANES), jnp.float32)

    inner = pl.ds(LANES, tiles * LANES)

    @pl.when(jnp.logical_not(has_up))
    def _():
        top_in[:, :, inner] = jnp.zeros((planes, HALO, tiles * LANES), xin.dtype)

    @pl.when(jnp.logical_not(has_down))
    def _():
        bot_in[:, :, inner] = jnp.zeros((planes, HALO, tiles * LANES), xin.dtype)

    for part, (start, size) in enumerate(parts):
        load(part).wait()

        @pl.loop(0, planes)
        def _(p):
            top_out[p, :, cols(start, size)] = xin[p, 0:HALO, cols(start + 1, size)]
            bot_out[p, :, cols(start, size)] = xin[p, rows - HALO : rows, cols(start + 1, size)]

        if part == 0:
            neighbours = jnp.where(has_up, 1, 0) + jnp.where(has_down, 1, 0) + gz_count - 1
            pl.semaphore_wait(barrier, neighbours)

        @pl.when(has_up)
        def _():
            to_up(part).start()

        @pl.when(has_down)
        def _():
            to_down(part).start()

    tall = rows + 8
    lane_tall = lax.broadcasted_iota(jnp.int32, (tall, LANES), 1)
    lane = lax.broadcasted_iota(jnp.int32, (rows, LANES), 1)
    row_tall = lax.broadcasted_iota(jnp.int32, (tall, LANES), 0)
    first = jnp.where(has_up, 0, 2)
    last = jnp.where(has_down, rows + 4, rows + 2)
    row_mask = jnp.where((row_tall >= first) & (row_tall < last), 1.0, 0.0).astype(jnp.float32)

    def scores(chunk, e_start, e_count):
        @pl.loop(0, planes)
        def _(p):
            for i in range(e_count + 2):
                here = cols(e_start + i, 1)
                xs[i, 8 : 8 + rows, :] = xin[p, :, here].astype(jnp.float32)
                xs[i, 4:8, :] = top_in[p, :, here].astype(jnp.float32)
                xs[i, 8 + rows : 12 + rows, :] = bot_in[p, :, here].astype(jnp.float32)
            mid, smooth = [], []
            for i in range(e_count + 2):
                centre = xs[i, 6 : 6 + tall, :]
                mid.append(centre)
                smooth.append(
                    xs[i, 5 : 5 + tall, :] + xs[i, 7 : 7 + tall, :] + (centre + centre)
                )
            right = from_right(smooth, 1, lane_tall)
            pair = [smooth[i] + right[i] for i in range(e_count + 1)]
            left = from_left(pair, 1, lane_tall)
            left2 = from_left(mid, 2, lane_tall)
            right2 = from_right(mid, 2, lane_tall)
            for i in range(e_count):
                total = pair[i + 1] + left[i]
                total = total + (left2[i] + right2[i + 1])
                total = total + (xs[i + 1, 4 : 4 + tall, :] + xs[i + 1, 8 : 8 + tall, :])
                laplace = 20.0 * mid[i + 1] - total
                es[i, :, :] = laplace * laplace * row_mask
            for i in range(e_count):
                column = es[i, 0:rows, :]
                for k in range(1, 5):
                    column = column + es[i, k : k + rows, :]
                vs[p, e_start + i + 1] = column
            flat = [vs[p, chunk * own_tiles + i] for i in range(own_tiles + 2)]
            right = from_right(flat, 1, lane)
            pair = [flat[i] + right[i] for i in range(own_tiles + 1)]
            left = from_left(pair, 2, lane)
            right2 = from_right(flat, 2, lane)
            for i in range(own_tiles):
                ss[p, i] = (pair[i + 1] + left[i] + right2[i + 1]) * sharpness

    def finish(chunk, tile, dst):
        peak = ss[0, tile]
        for p in range(1, planes):
            peak = jnp.maximum(peak, ss[p, tile])
        here = cols(chunk * own_tiles + tile + 1, 1)
        total, blend = None, None
        for p in range(planes):
            weight = jnp.exp(ss[p, tile] - peak)
            term = weight * xin[p, :, here].astype(jnp.float32)
            total = weight if total is None else total + weight
            blend = term if blend is None else blend + term
        dst[0] = peak + jnp.log(total)
        dst[1] = blend / total

    group_tiles = own_tiles // groups

    def to_peer(step, group):
        part = pl.ds(group * group_tiles, group_tiles)
        return pltpu.make_async_remote_copy(
            src_ref=outbox.at[step, part], dst_ref=inbox.at[step, part],
            send_sem=gz_send.at[step, group], recv_sem=gz_recv.at[step, group],
            device_id={"gz": lax.rem(gz + 1 + step, gz_count)}, device_id_type=MESH,
        )

    def halo_arrived(part):
        @pl.when(has_down)
        def _():
            to_up(part).wait_recv()

        @pl.when(has_up)
        def _():
            to_down(part).wait_recv()

    for step in range(gz_count):
        chunk = lax.rem(gz + 1 + step, gz_count)
        if step < len(parts):
            halo_arrived(step)
        if gz_count == 2:
            if step == 0:
                e_start, e_count = jnp.where(gz == 0, tiles - own_tiles - 1, 0), own_tiles + 1
            else:
                e_start, e_count = jnp.where(gz == 0, 0, own_tiles + 1), own_tiles - 1
        else:
            e_count = own_tiles + 2
            e_start = jnp.clip(chunk * own_tiles - 1, 0, tiles - e_count)
        scores(chunk, e_start, e_count)
        if step < gz_count - 1:
            for group in range(groups):
                @pl.loop(group * group_tiles, (group + 1) * group_tiles)
                def _(tile):
                    finish(chunk, tile, outbox.at[step, tile])

                to_peer(step, group).start()
        else:
            @pl.loop(0, own_tiles)
            def _(tile):
                finish(chunk, tile, own.at[tile])

    for group in range(groups):
        for step in range(gz_count - 1):
            to_peer(step, group).wait()
        for tile in range(group * group_tiles, (group + 1) * group_tiles):
            logs = [own[tile, 0]] + [inbox[s, tile, 0] for s in range(gz_count - 1)]
            means = [own[tile, 1]] + [inbox[s, tile, 1] for s in range(gz_count - 1)]
            peak = functools.reduce(jnp.maximum, logs)
            shares = [jnp.exp(value - peak) for value in logs]
            blend = sum(share * mean for share, mean in zip(shares, means))
            joined = blend / sum(shares)
            joined_ref[:, tile * LANES : (tile + 1) * LANES] = joined
            jt[tile] = joined

    half = rows // 2
    source = lax.broadcasted_iota(jnp.int32, (2 * LANES, LANES), 0)
    target = lax.broadcasted_iota(jnp.int32, (2 * LANES, LANES), 1)
    gather = jnp.where(lax.div(source, 2) == target, 0.25, 0.0).astype(jnp.float32)
    for pair_index in range(own_tiles // 2):
        sides = []
        for tile in (2 * pair_index, 2 * pair_index + 1):
            sides.append(
                jt[tile, pl.ds(0, half, stride=2), :] + jt[tile, pl.ds(1, half, stride=2), :]
            )
        wide = jnp.concatenate(sides, axis=1)
        pooled_ref[:, pair_index * LANES : (pair_index + 1) * LANES] = jnp.dot(
            wide, gather, precision=lax.Precision.HIGHEST, preferred_element_type=jnp.float32
        )

    for part in range(len(parts)):
        @pl.when(has_up)
        def _():
            to_up(part).wait_send()

        @pl.when(has_down)
        def _():
            to_down(part).wait_send()


def shards(gz_count, xy_count, stack):
    planes, rows, breadth = stack.shape
    tiles = breadth // LANES
    own_tiles = tiles // gz_count
    groups = 2
    geom = (planes, rows, tiles, gz_count, xy_count, own_tiles, groups)
    f32 = jnp.float32
    padded = breadth + 2 * LANES
    spread = own_tiles + 4
    parts = 2 if gz_count == 2 else 1
    return pl.pallas_call(
        functools.partial(kernel, geom),
        out_shape=(
            jax.ShapeDtypeStruct((rows, own_tiles * LANES), f32),
            jax.ShapeDtypeStruct((rows // 2, own_tiles * LANES // 2), f32),
        ),
        in_specs=[pl.BlockSpec(memory_space=pl.ANY)],
        out_specs=(
            pl.BlockSpec(memory_space=pltpu.VMEM),
            pl.BlockSpec(memory_space=pltpu.VMEM),
        ),
        scratch_shapes=[
            pltpu.VMEM((planes, rows, padded), stack.dtype),
            pltpu.VMEM((planes, HALO, padded), stack.dtype),
            pltpu.VMEM((planes, HALO, padded), stack.dtype),
            pltpu.VMEM((planes, HALO, breadth), stack.dtype),
            pltpu.VMEM((planes, HALO, breadth), stack.dtype),
            pltpu.VMEM((spread, rows + 16, LANES), f32),
            pltpu.VMEM((spread, rows + 8, LANES), f32),
            pltpu.VMEM((planes, tiles + 2, rows, LANES), f32),
            pltpu.VMEM((planes, own_tiles, rows, LANES), f32),
            pltpu.VMEM((own_tiles, 2, rows, LANES), f32),
            pltpu.VMEM((gz_count - 1, own_tiles, 2, rows, LANES), f32),
            pltpu.VMEM((gz_count - 1, own_tiles, 2, rows, LANES), f32),
            pltpu.VMEM((own_tiles, rows, LANES), f32),
            pltpu.SemaphoreType.DMA((parts,)),
            pltpu.SemaphoreType.DMA((2, parts)),
            pltpu.SemaphoreType.DMA((2, parts)),
            pltpu.SemaphoreType.DMA((gz_count - 1, groups)),
            pltpu.SemaphoreType.DMA((gz_count - 1, groups)),
        ],
        compiler_params=pltpu.CompilerParams(collective_id=0, has_side_effects=True),
    )(stack)


def solution(mesh):
    body = functools.partial(shards, mesh.shape["gz"], mesh.shape["xy"])
    in_specs = (P("gz", "xy", None),)
    out_specs = (P("xy", "gz"), P("xy", "gz"))
    return jax.shard_map(body, mesh=mesh, in_specs=in_specs, out_specs=out_specs, check_vma=False)
```

```python
import functools

import jax
import jax.numpy as jnp
from jax import lax
from jax.experimental import pallas as pl
from jax.experimental.pallas import tpu as pltpu
from jax.sharding import PartitionSpec as P

sharpness = 0.016
LANES = 128
HALO = 4
MESH = pl.DeviceIdType.MESH


def cols(tile, count):
    return pl.ds(pl.multiple_of(tile * LANES, LANES), count * LANES)


def from_left(tiles, step, lane):
    rolled = [pltpu.roll(t, step, 1) for t in tiles]
    return [jnp.where(lane < step, rolled[i], rolled[i + 1]) for i in range(len(tiles) - 1)]


def from_right(tiles, step, lane):
    rolled = [pltpu.roll(t, LANES - step, 1) for t in tiles]
    return [
        jnp.where(lane < LANES - step, rolled[i], rolled[i + 1]) for i in range(len(tiles) - 1)
    ]


def kernel(
    geom, x_hbm, joined_ref, pooled_ref,
    xin, top_in, bot_in, top_out, bot_out, taps, xs, gs, hs, es, vs, ss, own, outbox, inbox, jt,
    load_sem, halo_send, halo_recv, gz_send, gz_recv,
):
    planes, rows, tiles, gz_count, xy_count, own_tiles, groups = geom
    gz = lax.axis_index("gz")
    xy = lax.axis_index("xy")
    has_up = xy > 0
    has_down = xy < xy_count - 1

    if gz_count == 2:
        near = own_tiles + 2
        parts = [
            (jnp.where(gz == 0, tiles - near, 0), near),
            (jnp.where(gz == 0, 0, near), tiles - near),
        ]
    else:
        parts = [(0, tiles)]

    def load(part):
        start, size = parts[part]
        return pltpu.make_async_copy(
            x_hbm.at[:, :, cols(start, size)], xin.at[:, :, cols(start + 1, size)], load_sem.at[part]
        )

    for part in range(len(parts)):
        load(part).start()

    barrier = pltpu.get_barrier_semaphore()

    @pl.when(has_up)
    def _():
        pl.semaphore_signal(barrier, inc=1, device_id={"xy": xy - 1}, device_id_type=MESH)

    @pl.when(has_down)
    def _():
        pl.semaphore_signal(barrier, inc=1, device_id={"xy": xy + 1}, device_id_type=MESH)

    for step in range(gz_count - 1):
        peer = lax.rem(gz + 1 + step, gz_count)
        pl.semaphore_signal(barrier, inc=1, device_id={"gz": peer}, device_id_type=MESH)

    def to_up(part):
        start, size = parts[part]
        return pltpu.make_async_remote_copy(
            src_ref=top_out.at[:, cols(start, size)],
            dst_ref=bot_in.at[:, cols(start + 1, size)],
            send_sem=halo_send.at[0, part], recv_sem=halo_recv.at[0, part],
            device_id={"xy": xy - 1}, device_id_type=MESH,
        )

    def to_down(part):
        start, size = parts[part]
        return pltpu.make_async_remote_copy(
            src_ref=bot_out.at[:, cols(start, size)],
            dst_ref=top_in.at[:, cols(start + 1, size)],
            send_sem=halo_send.at[1, part], recv_sem=halo_recv.at[1, part],
            device_id={"xy": xy + 1}, device_id_type=MESH,
        )

    edge = HALO * planes
    for tile in (0, tiles + 1):
        side = pl.ds(tile * LANES, LANES)
        xin[:, :, side] = jnp.zeros((planes, rows, LANES), xin.dtype)
        top_in[:, side] = jnp.zeros((edge, LANES), xin.dtype)
        bot_in[:, side] = jnp.zeros((edge, LANES), xin.dtype)
        vs[:, tile] = jnp.zeros((planes, rows, LANES), jnp.float32)

    inner = pl.ds(LANES, tiles * LANES)

    @pl.when(jnp.logical_not(has_up))
    def _():
        top_in[:, inner] = jnp.zeros((edge, tiles * LANES), xin.dtype)

    @pl.when(jnp.logical_not(has_down))
    def _():
        bot_in[:, inner] = jnp.zeros((edge, tiles * LANES), xin.dtype)

    low = lax.broadcasted_iota(jnp.int32, (8, LANES), 0) < HALO
    for part, (start, size) in enumerate(parts):
        load(part).wait()

        @pl.loop(start, start + size)
        def _(t):
            here = cols(t + 1, 1)
            for p in range(planes):
                xs[t, p, 8 : 8 + rows, :] = xin[p, :, here].astype(jnp.float32)
            out = cols(t, 1)
            for quad in range(planes // 4):
                tops, bots = [], []
                for p in (4 * quad, 4 * quad + 2):
                    tops.append(jnp.where(low, xs[t, p, 8:16, :], xs[t, p + 1, 4:12, :]))
                    bots.append(
                        jnp.where(
                            low,
                            xs[t, p, 4 + rows : 12 + rows, :],
                            xs[t, p + 1, rows : 8 + rows, :],
                        )
                    )
                place = slice(16 * quad, 16 * quad + 16)
                top_out[place, out] = jnp.concatenate(tops, axis=0).astype(xin.dtype)
                bot_out[place, out] = jnp.concatenate(bots, axis=0).astype(xin.dtype)

        if part == 0:
            neighbours = jnp.where(has_up, 1, 0) + jnp.where(has_down, 1, 0) + gz_count - 1
            pl.semaphore_wait(barrier, neighbours)

        @pl.when(has_up)
        def _():
            to_up(part).start()

        @pl.when(has_down)
        def _():
            to_down(part).start()

    source = lax.broadcasted_iota(jnp.int32, (3 * LANES, LANES), 0)
    target = lax.broadcasted_iota(jnp.int32, (3 * LANES, LANES), 1)
    apart = jnp.abs(source - target - LANES)
    centre = jnp.where(apart == 0, 16.0, jnp.where(apart == 1, -2.0, jnp.where(apart == 2, -1.0, 0.0)))
    beside = jnp.where(apart == 0, -2.0, jnp.where(apart == 1, -1.0, 0.0))
    taps[:, 0:LANES] = centre.astype(taps.dtype)
    taps[:, LANES : 2 * LANES] = beside.astype(taps.dtype)

    @pl.loop(0, tiles)
    def _(t):
        wide = xin[:, :, cols(t, 3)].reshape(planes * rows, 3 * LANES)
        both = jnp.dot(wide, taps[...], preferred_element_type=jnp.float32)
        both = both.reshape(planes, rows, 2 * LANES)
        hs[t, :, 8 : 8 + rows, :] = both[:, :, 0:LANES]
        gs[t, :, 8 : 8 + rows, :] = both[:, :, LANES:]

    tall = rows + 8
    lane = lax.broadcasted_iota(jnp.int32, (rows, LANES), 1)
    row_tall = lax.broadcasted_iota(jnp.int32, (tall, LANES), 0)
    first = jnp.where(has_up, 0, 2)
    last = jnp.where(has_down, rows + 4, rows + 2)
    row_mask = jnp.where((row_tall >= first) & (row_tall < last), 1.0, 0.0).astype(jnp.float32)

    def scores(chunk, e_start, e_count):
        @pl.loop(e_start, e_start + e_count)
        def _(t):
            for ref, base in ((top_in, 4), (bot_in, 8 + rows)):
                both = jnp.dot(
                    ref[:, cols(t, 3)], taps[...], preferred_element_type=jnp.float32
                )
                plain = ref[:, cols(t + 1, 1)].astype(jnp.float32)
                for p in range(planes):
                    part = slice(HALO * p, HALO * p + HALO)
                    hs[t, p, base : base + HALO, :] = both[part, 0:LANES]
                    gs[t, p, base : base + HALO, :] = both[part, LANES:]
                    xs[t, p, base : base + HALO, :] = plain[part, :]

        @pl.loop(0, planes)
        def _(p):
            for i in range(e_count):
                t = e_start + i
                laplace = (
                    hs[t, p, 6 : 6 + tall, :]
                    + (gs[t, p, 5 : 5 + tall, :] + gs[t, p, 7 : 7 + tall, :])
                    - (xs[t, p, 4 : 4 + tall, :] + xs[t, p, 8 : 8 + tall, :])
                )
                es[i, :, :] = laplace * laplace * row_mask
            for i in range(e_count):
                column = es[i, 0:rows, :]
                for k in range(1, 5):
                    column = column + es[i, k : k + rows, :]
                vs[p, e_start + i + 1] = column
            flat = [vs[p, chunk * own_tiles + i] for i in range(own_tiles + 2)]
            right = from_right(flat, 1, lane)
            pair = [flat[i] + right[i] for i in range(own_tiles + 1)]
            left = from_left(pair, 2, lane)
            right2 = from_right(flat, 2, lane)
            for i in range(own_tiles):
                ss[p, i] = (pair[i + 1] + left[i] + right2[i + 1]) * sharpness

    def finish(chunk, tile, dst):
        peak = ss[0, tile]
        for p in range(1, planes):
            peak = jnp.maximum(peak, ss[p, tile])
        place = chunk * own_tiles + tile
        total, blend = None, None
        for p in range(planes):
            weight = jnp.exp(ss[p, tile] - peak)
            term = weight * xs[place, p, 8 : 8 + rows, :]
            total = weight if total is None else total + weight
            blend = term if blend is None else blend + term
        dst[0] = peak + jnp.log(total)
        dst[1] = blend / total

    group_tiles = own_tiles // groups

    def to_peer(step, group):
        part = pl.ds(group * group_tiles, group_tiles)
        return pltpu.make_async_remote_copy(
            src_ref=outbox.at[step, part], dst_ref=inbox.at[step, part],
            send_sem=gz_send.at[step, group], recv_sem=gz_recv.at[step, group],
            device_id={"gz": lax.rem(gz + 1 + step, gz_count)}, device_id_type=MESH,
        )

    def halo_arrived(part):
        @pl.when(has_down)
        def _():
            to_up(part).wait_recv()

        @pl.when(has_up)
        def _():
            to_down(part).wait_recv()

    for step in range(gz_count):
        chunk = lax.rem(gz + 1 + step, gz_count)
        if step < len(parts):
            halo_arrived(step)
        if gz_count == 2:
            if step == 0:
                e_start, e_count = jnp.where(gz == 0, tiles - own_tiles - 1, 0), own_tiles + 1
            else:
                e_start, e_count = jnp.where(gz == 0, 0, own_tiles + 1), own_tiles - 1
        else:
            e_count = own_tiles + 2
            e_start = jnp.clip(chunk * own_tiles - 1, 0, tiles - e_count)
        scores(chunk, e_start, e_count)
        if step < gz_count - 1:
            for group in range(groups):
                @pl.loop(group * group_tiles, (group + 1) * group_tiles)
                def _(tile):
                    finish(chunk, tile, outbox.at[step, tile])

                to_peer(step, group).start()
        else:
            @pl.loop(0, own_tiles)
            def _(tile):
                finish(chunk, tile, own.at[tile])

    for group in range(groups):
        for step in range(gz_count - 1):
            to_peer(step, group).wait()
        for tile in range(group * group_tiles, (group + 1) * group_tiles):
            logs = [own[tile, 0]] + [inbox[s, tile, 0] for s in range(gz_count - 1)]
            means = [own[tile, 1]] + [inbox[s, tile, 1] for s in range(gz_count - 1)]
            peak = functools.reduce(jnp.maximum, logs)
            shares = [jnp.exp(value - peak) for value in logs]
            blend = sum(share * mean for share, mean in zip(shares, means))
            joined = blend / sum(shares)
            joined_ref[:, tile * LANES : (tile + 1) * LANES] = joined
            jt[tile] = joined

    half = rows // 2
    source = lax.broadcasted_iota(jnp.int32, (2 * LANES, LANES), 0)
    target = lax.broadcasted_iota(jnp.int32, (2 * LANES, LANES), 1)
    gather = jnp.where(lax.div(source, 2) == target, 0.25, 0.0).astype(jnp.float32)
    for pair_index in range(own_tiles // 2):
        sides = []
        for tile in (2 * pair_index, 2 * pair_index + 1):
            sides.append(
                jt[tile, pl.ds(0, half, stride=2), :] + jt[tile, pl.ds(1, half, stride=2), :]
            )
        wide = jnp.concatenate(sides, axis=1)
        pooled_ref[:, pair_index * LANES : (pair_index + 1) * LANES] = jnp.dot(
            wide, gather, precision=lax.Precision.HIGHEST, preferred_element_type=jnp.float32
        )

    for part in range(len(parts)):
        @pl.when(has_up)
        def _():
            to_up(part).wait_send()

        @pl.when(has_down)
        def _():
            to_down(part).wait_send()


def shards(gz_count, xy_count, stack):
    planes, rows, breadth = stack.shape
    tiles = breadth // LANES
    own_tiles = tiles // gz_count
    groups = 2
    geom = (planes, rows, tiles, gz_count, xy_count, own_tiles, groups)
    f32 = jnp.float32
    padded = breadth + 2 * LANES
    spread = own_tiles + 4
    parts = 2 if gz_count == 2 else 1
    return pl.pallas_call(
        functools.partial(kernel, geom),
        out_shape=(
            jax.ShapeDtypeStruct((rows, own_tiles * LANES), f32),
            jax.ShapeDtypeStruct((rows // 2, own_tiles * LANES // 2), f32),
        ),
        in_specs=[pl.BlockSpec(memory_space=pltpu.HBM)],
        out_specs=(
            pl.BlockSpec(memory_space=pltpu.VMEM),
            pl.BlockSpec(memory_space=pltpu.VMEM),
        ),
        scratch_shapes=[
            pltpu.VMEM((planes, rows, padded), stack.dtype),
            pltpu.VMEM((planes * HALO, padded), stack.dtype),
            pltpu.VMEM((planes * HALO, padded), stack.dtype),
            pltpu.VMEM((planes * HALO, breadth), stack.dtype),
            pltpu.VMEM((planes * HALO, breadth), stack.dtype),
            pltpu.VMEM((3 * LANES, 2 * LANES), stack.dtype),
            pltpu.VMEM((tiles, planes, rows + 16, LANES), f32),
            pltpu.VMEM((tiles, planes, rows + 16, LANES), f32),
            pltpu.VMEM((tiles, planes, rows + 16, LANES), f32),
            pltpu.VMEM((spread, rows + 8, LANES), f32),
            pltpu.VMEM((planes, tiles + 2, rows, LANES), f32),
            pltpu.VMEM((planes, own_tiles, rows, LANES), f32),
            pltpu.VMEM((own_tiles, 2, rows, LANES), f32),
            pltpu.VMEM((gz_count - 1, own_tiles, 2, rows, LANES), f32),
            pltpu.VMEM((gz_count - 1, own_tiles, 2, rows, LANES), f32),
            pltpu.VMEM((own_tiles, rows, LANES), f32),
            pltpu.SemaphoreType.DMA((parts,)),
            pltpu.SemaphoreType.DMA((2, parts)),
            pltpu.SemaphoreType.DMA((2, parts)),
            pltpu.SemaphoreType.DMA((gz_count - 1, groups)),
            pltpu.SemaphoreType.DMA((gz_count - 1, groups)),
        ],
        compiler_params=pltpu.CompilerParams(collective_id=0, has_side_effects=True, vmem_limit_bytes=28 * 2**20),
    )(stack)


def solution(mesh):
    body = functools.partial(shards, mesh.shape["gz"], mesh.shape["xy"])
    in_specs = (P("gz", "xy", None),)
    out_specs = (P("xy", "gz"), P("xy", "gz"))
    return jax.shard_map(body, mesh=mesh, in_specs=in_specs, out_specs=out_specs, check_vma=False)
```

```python
import functools

import jax
import jax.numpy as jnp
from jax import lax
from jax.experimental import pallas as pl
from jax.experimental.pallas import tpu as pltpu
from jax.sharding import PartitionSpec as P

sharpness = 0.016
LANES = 128
HALO = 4
VMEM_GRANT = 67043328 - 15 * 2**16
MESH = pl.DeviceIdType.MESH


def cols(tile, count):
    return pl.ds(pl.multiple_of(tile * LANES, LANES), count * LANES)


def each(start, count, body, width=2):
    @pl.loop(0, count // width)
    def _(turn):
        for k in range(width):
            body(start + turn * width + k)

    for k in range(count - count % width, count):
        body(start + k)


def from_left(tiles, step, lane):
    rolled = [pltpu.roll(t, step, 1) for t in tiles]
    return [jnp.where(lane < step, rolled[i], rolled[i + 1]) for i in range(len(tiles) - 1)]


def from_right(tiles, step, lane):
    rolled = [pltpu.roll(t, LANES - step, 1) for t in tiles]
    return [
        jnp.where(lane < LANES - step, rolled[i], rolled[i + 1]) for i in range(len(tiles) - 1)
    ]


def kernel(
    geom, x_hbm, joined_ref, pooled_ref,
    xin, top_in, bot_in, top_out, bot_out, taps, xs, gs, hs, es, vs, ss, own, outbox, inbox, jt,
    load_sem, halo_send, halo_recv, gz_send, gz_recv,
):
    planes, rows, tiles, gz_count, xy_count, own_tiles, groups = geom
    gz = lax.axis_index("gz")
    xy = lax.axis_index("xy")
    has_up = xy > 0
    has_down = xy < xy_count - 1

    if gz_count == 2:
        near = own_tiles + 2
        parts = [
            (jnp.where(gz == 0, tiles - near, 0), near),
            (jnp.where(gz == 0, 0, near), tiles - near),
        ]
    else:
        parts = [(0, tiles)]

    def load(part):
        start, size = parts[part]
        return pltpu.make_async_copy(
            x_hbm.at[:, :, cols(start, size)], xin.at[:, :, cols(start + 1, size)], load_sem.at[part]
        )

    for part in range(len(parts)):
        load(part).start()

    barrier = pltpu.get_barrier_semaphore()

    @pl.when(has_up)
    def _():
        pl.semaphore_signal(barrier, inc=1, device_id={"xy": xy - 1}, device_id_type=MESH)

    @pl.when(has_down)
    def _():
        pl.semaphore_signal(barrier, inc=1, device_id={"xy": xy + 1}, device_id_type=MESH)

    for step in range(gz_count - 1):
        peer = lax.rem(gz + 1 + step, gz_count)
        pl.semaphore_signal(barrier, inc=1, device_id={"gz": peer}, device_id_type=MESH)

    def to_up(part):
        start, size = parts[part]
        return pltpu.make_async_remote_copy(
            src_ref=top_out.at[:, cols(start, size)],
            dst_ref=bot_in.at[:, cols(start + 1, size)],
            send_sem=halo_send.at[0, part], recv_sem=halo_recv.at[0, part],
            device_id={"xy": xy - 1}, device_id_type=MESH,
        )

    def to_down(part):
        start, size = parts[part]
        return pltpu.make_async_remote_copy(
            src_ref=bot_out.at[:, cols(start, size)],
            dst_ref=top_in.at[:, cols(start + 1, size)],
            send_sem=halo_send.at[1, part], recv_sem=halo_recv.at[1, part],
            device_id={"xy": xy + 1}, device_id_type=MESH,
        )

    edge = HALO * planes
    for tile in (0, tiles + 1):
        side = pl.ds(tile * LANES, LANES)
        xin[:, :, side] = jnp.zeros((planes, rows, LANES), xin.dtype)
        top_in[:, side] = jnp.zeros((edge, LANES), xin.dtype)
        bot_in[:, side] = jnp.zeros((edge, LANES), xin.dtype)
        vs[:, tile] = jnp.zeros((planes, rows, LANES), jnp.float32)

    inner = pl.ds(LANES, tiles * LANES)

    @pl.when(jnp.logical_not(has_up))
    def _():
        top_in[:, inner] = jnp.zeros((edge, tiles * LANES), xin.dtype)

    @pl.when(jnp.logical_not(has_down))
    def _():
        bot_in[:, inner] = jnp.zeros((edge, tiles * LANES), xin.dtype)

    low = lax.broadcasted_iota(jnp.int32, (8, LANES), 0) < HALO
    for part, (start, size) in enumerate(parts):
        load(part).wait()

        @pl.loop(start, start + size)
        def _(t):
            here = cols(t + 1, 1)
            for p in range(planes):
                xs[t, p, 8 : 8 + rows, :] = xin[p, :, here].astype(jnp.float32)
            out = cols(t, 1)
            for quad in range(planes // 4):
                tops, bots = [], []
                for p in (4 * quad, 4 * quad + 2):
                    tops.append(jnp.where(low, xs[t, p, 8:16, :], xs[t, p + 1, 4:12, :]))
                    bots.append(
                        jnp.where(
                            low,
                            xs[t, p, 4 + rows : 12 + rows, :],
                            xs[t, p + 1, rows : 8 + rows, :],
                        )
                    )
                place = slice(16 * quad, 16 * quad + 16)
                top_out[place, out] = jnp.concatenate(tops, axis=0).astype(xin.dtype)
                bot_out[place, out] = jnp.concatenate(bots, axis=0).astype(xin.dtype)

        if part == 0:
            neighbours = jnp.where(has_up, 1, 0) + jnp.where(has_down, 1, 0) + gz_count - 1
            pl.semaphore_wait(barrier, neighbours)

        @pl.when(has_up)
        def _():
            to_up(part).start()

        @pl.when(has_down)
        def _():
            to_down(part).start()

    source = lax.broadcasted_iota(jnp.int32, (3 * LANES, LANES), 0)
    target = lax.broadcasted_iota(jnp.int32, (3 * LANES, LANES), 1)
    apart = jnp.abs(source - target - LANES)
    centre = jnp.where(apart == 0, 16.0, jnp.where(apart == 1, -2.0, jnp.where(apart == 2, -1.0, 0.0)))
    beside = jnp.where(apart == 0, -2.0, jnp.where(apart == 1, -1.0, 0.0))
    taps[:, 0:LANES] = centre.astype(taps.dtype)
    taps[:, LANES : 2 * LANES] = beside.astype(taps.dtype)

    def own_taps(t):
        wide = xin[:, :, cols(t, 3)].reshape(planes * rows, 3 * LANES)
        both = jnp.dot(wide, taps[...], preferred_element_type=jnp.float32)
        both = both.reshape(planes, rows, 2 * LANES)
        hs[t, :, 8 : 8 + rows, :] = both[:, :, 0:LANES]
        gs[t, :, 8 : 8 + rows, :] = both[:, :, LANES:]

    each(0, tiles, own_taps)

    tall = rows + 8
    lane = lax.broadcasted_iota(jnp.int32, (rows, LANES), 1)
    row_tall = lax.broadcasted_iota(jnp.int32, (tall, LANES), 0)
    first = jnp.where(has_up, 0, 2)
    last = jnp.where(has_down, rows + 4, rows + 2)
    row_mask = jnp.where((row_tall >= first) & (row_tall < last), 1.0, 0.0).astype(jnp.float32)

    def scores(chunk, e_start, e_count):
        def halo_taps(turn, width):
            first_tile = e_start + turn
            wide = [
                ref[:, cols(first_tile + k, 3)] for k in range(width) for ref in (top_in, bot_in)
            ]
            both = jnp.dot(
                jnp.concatenate(wide, axis=0), taps[...], preferred_element_type=jnp.float32
            )
            for k in range(width):
                t = first_tile + k
                for side, (ref, base) in enumerate(((top_in, 4), (bot_in, 8 + rows))):
                    plain = ref[:, cols(t + 1, 1)].astype(jnp.float32)
                    for p in range(planes):
                        part = slice(HALO * p, HALO * p + HALO)
                        row = (2 * k + side) * edge + HALO * p
                        hs[t, p, base : base + HALO, :] = both[row : row + HALO, 0:LANES]
                        gs[t, p, base : base + HALO, :] = both[row : row + HALO, LANES:]
                        xs[t, p, base : base + HALO, :] = plain[part, :]

        width = 3

        @pl.loop(0, e_count // width)
        def _(turn):
            halo_taps(turn * width, width)

        if e_count % width:
            halo_taps(e_count - e_count % width, e_count % width)

        @pl.loop(0, planes // 2)
        def _(turn):
            pair_of = [(2 * turn, 0), (2 * turn + 1, 1)]
            for p, bank in pair_of:
                for i in range(e_count):
                    t = e_start + i
                    laplace = (
                        hs[t, p, 6 : 6 + tall, :]
                        + (gs[t, p, 5 : 5 + tall, :] + gs[t, p, 7 : 7 + tall, :])
                        - (xs[t, p, 4 : 4 + tall, :] + xs[t, p, 8 : 8 + tall, :])
                    )
                    es[bank, i, :, :] = laplace * laplace * row_mask
            for p, bank in pair_of:
                for i in range(e_count):
                    column = es[bank, i, 0:rows, :]
                    for k in range(1, 5):
                        column = column + es[bank, i, k : k + rows, :]
                    vs[p, e_start + i + 1] = column
            for p, bank in pair_of:
                flat = [vs[p, chunk * own_tiles + i] for i in range(own_tiles + 2)]
                right = from_right(flat, 1, lane)
                pair = [flat[i] + right[i] for i in range(own_tiles + 1)]
                left = from_left(pair, 2, lane)
                right2 = from_right(flat, 2, lane)
                for i in range(own_tiles):
                    ss[p, i] = (pair[i + 1] + left[i] + right2[i + 1]) * sharpness

    def finish(chunk, tile, dst):
        peak = ss[0, tile]
        for p in range(1, planes):
            peak = jnp.maximum(peak, ss[p, tile])
        place = chunk * own_tiles + tile
        total, blend = None, None
        for p in range(planes):
            weight = jnp.exp(ss[p, tile] - peak)
            term = weight * xs[place, p, 8 : 8 + rows, :]
            total = weight if total is None else total + weight
            blend = term if blend is None else blend + term
        dst[0] = peak + jnp.log(total)
        dst[1] = blend / total

    group_tiles = own_tiles // groups

    def to_peer(step, group):
        part = pl.ds(group * group_tiles, group_tiles)
        return pltpu.make_async_remote_copy(
            src_ref=outbox.at[step, part], dst_ref=inbox.at[step, part],
            send_sem=gz_send.at[step, group], recv_sem=gz_recv.at[step, group],
            device_id={"gz": lax.rem(gz + 1 + step, gz_count)}, device_id_type=MESH,
        )

    def halo_arrived(part):
        @pl.when(has_down)
        def _():
            to_up(part).wait_recv()

        @pl.when(has_up)
        def _():
            to_down(part).wait_recv()

    for step in range(gz_count):
        chunk = lax.rem(gz + 1 + step, gz_count)
        if step < len(parts):
            halo_arrived(step)
        if gz_count == 2:
            if step == 0:
                e_start, e_count = jnp.where(gz == 0, tiles - own_tiles - 1, 0), own_tiles + 1
            else:
                e_start, e_count = jnp.where(gz == 0, 0, own_tiles + 1), own_tiles - 1
        else:
            e_count = own_tiles + 2
            e_start = jnp.clip(chunk * own_tiles - 1, 0, tiles - e_count)
        scores(chunk, e_start, e_count)
        if step < gz_count - 1:
            for group in range(groups):
                each(
                    group * group_tiles, group_tiles,
                    lambda tile: finish(chunk, tile, outbox.at[step, tile]),
                )
                to_peer(step, group).start()
        else:
            each(0, own_tiles, lambda tile: finish(chunk, tile, own.at[tile]))

    for group in range(groups):
        for step in range(gz_count - 1):
            to_peer(step, group).wait()
        for tile in range(group * group_tiles, (group + 1) * group_tiles):
            logs = [own[tile, 0]] + [inbox[s, tile, 0] for s in range(gz_count - 1)]
            means = [own[tile, 1]] + [inbox[s, tile, 1] for s in range(gz_count - 1)]
            peak = functools.reduce(jnp.maximum, logs)
            shares = [jnp.exp(value - peak) for value in logs]
            blend = sum(share * mean for share, mean in zip(shares, means))
            joined = blend / sum(shares)
            joined_ref[:, tile * LANES : (tile + 1) * LANES] = joined
            jt[tile] = joined

    half = rows // 2
    source = lax.broadcasted_iota(jnp.int32, (2 * LANES, LANES), 0)
    target = lax.broadcasted_iota(jnp.int32, (2 * LANES, LANES), 1)
    gather = jnp.where(lax.div(source, 2) == target, 0.25, 0.0).astype(jnp.float32)
    for pair_index in range(own_tiles // 2):
        sides = []
        for tile in (2 * pair_index, 2 * pair_index + 1):
            sides.append(
                jt[tile, pl.ds(0, half, stride=2), :] + jt[tile, pl.ds(1, half, stride=2), :]
            )
        wide = jnp.concatenate(sides, axis=1)
        pooled_ref[:, pair_index * LANES : (pair_index + 1) * LANES] = jnp.dot(
            wide, gather, precision=lax.Precision.HIGHEST, preferred_element_type=jnp.float32
        )

    for part in range(len(parts)):
        @pl.when(has_up)
        def _():
            to_up(part).wait_send()

        @pl.when(has_down)
        def _():
            to_down(part).wait_send()


def shards(gz_count, xy_count, stack):
    planes, rows, breadth = stack.shape
    tiles = breadth // LANES
    own_tiles = tiles // gz_count
    groups = 2
    geom = (planes, rows, tiles, gz_count, xy_count, own_tiles, groups)
    f32 = jnp.float32
    padded = breadth + 2 * LANES
    spread = own_tiles + 4
    parts = 2 if gz_count == 2 else 1
    return pl.pallas_call(
        functools.partial(kernel, geom),
        out_shape=(
            jax.ShapeDtypeStruct((rows, own_tiles * LANES), f32),
            jax.ShapeDtypeStruct((rows // 2, own_tiles * LANES // 2), f32),
        ),
        in_specs=[pl.BlockSpec(memory_space=pltpu.HBM)],
        out_specs=(
            pl.BlockSpec(memory_space=pltpu.VMEM),
            pl.BlockSpec(memory_space=pltpu.VMEM),
        ),
        scratch_shapes=[
            pltpu.VMEM((planes, rows, padded), stack.dtype),
            pltpu.VMEM((planes * HALO, padded), stack.dtype),
            pltpu.VMEM((planes * HALO, padded), stack.dtype),
            pltpu.VMEM((planes * HALO, breadth), stack.dtype),
            pltpu.VMEM((planes * HALO, breadth), stack.dtype),
            pltpu.VMEM((3 * LANES, 2 * LANES), stack.dtype),
            pltpu.VMEM((tiles, planes, rows + 16, LANES), f32),
            pltpu.VMEM((tiles, planes, rows + 16, LANES), f32),
            pltpu.VMEM((tiles, planes, rows + 16, LANES), f32),
            pltpu.VMEM((2, spread, rows + 8, LANES), f32),
            pltpu.VMEM((planes, tiles + 2, rows, LANES), f32),
            pltpu.VMEM((planes, own_tiles, rows, LANES), f32),
            pltpu.VMEM((own_tiles, 2, rows, LANES), f32),
            pltpu.VMEM((gz_count - 1, own_tiles, 2, rows, LANES), f32),
            pltpu.VMEM((gz_count - 1, own_tiles, 2, rows, LANES), f32),
            pltpu.VMEM((own_tiles, rows, LANES), f32),
            pltpu.SemaphoreType.DMA((parts,)),
            pltpu.SemaphoreType.DMA((2, parts)),
            pltpu.SemaphoreType.DMA((2, parts)),
            pltpu.SemaphoreType.DMA((gz_count - 1, groups)),
            pltpu.SemaphoreType.DMA((gz_count - 1, groups)),
        ],
        compiler_params=pltpu.CompilerParams(collective_id=0, has_side_effects=True, vmem_limit_bytes=VMEM_GRANT),
    )(stack)


def solution(mesh):
    body = functools.partial(shards, mesh.shape["gz"], mesh.shape["xy"])
    in_specs = (P("gz", "xy", None),)
    out_specs = (P("xy", "gz"), P("xy", "gz"))
    return jax.shard_map(body, mesh=mesh, in_specs=in_specs, out_specs=out_specs, check_vma=False)
```

```python
import functools

import jax
import jax.numpy as jnp
from jax import lax
from jax.experimental import pallas as pl
from jax.experimental.pallas import tpu as pltpu
from jax.sharding import PartitionSpec as P

sharpness = 0.016
LANES = 128
HALO = 4
VMEM_GRANT = 32 * 2**20
MESH = pl.DeviceIdType.MESH


def cols(tile, count):
    return pl.ds(pl.multiple_of(tile * LANES, LANES), count * LANES)


def each(start, count, body, width=2):
    @pl.loop(0, count // width)
    def _(turn):
        for k in range(width):
            body(start + turn * width + k)

    for k in range(count - count % width, count):
        body(start + k)


def from_left(tiles, step, lane):
    rolled = [pltpu.roll(t, step, 1) for t in tiles]
    return [jnp.where(lane < step, rolled[i], rolled[i + 1]) for i in range(len(tiles) - 1)]


def from_right(tiles, step, lane):
    rolled = [pltpu.roll(t, LANES - step, 1) for t in tiles]
    return [
        jnp.where(lane < LANES - step, rolled[i], rolled[i + 1]) for i in range(len(tiles) - 1)
    ]


def kernel(
    geom, x_hbm, joined_ref, pooled_ref,
    xin, top_in, bot_in, top_out, bot_out, taps, xs, gs, hs, es, vs, ss, own, outbox, inbox, jt,
    load_sem, halo_send, halo_recv, gz_send, gz_recv,
):
    planes, rows, tiles, gz_count, xy_count, own_tiles = geom
    gz = lax.axis_index("gz")
    xy = lax.axis_index("xy")
    has_up = xy > 0
    has_down = xy < xy_count - 1

    if gz_count == 2:
        piece = own_tiles // 2
        low_side = gz == 1

        def side(start, count):
            return jnp.where(low_side, start, tiles - start - count)

        sizes = [(0, piece + 2), (piece + 2, own_tiles - piece), (own_tiles + 2, own_tiles - 2)]
        parts = [(side(start, size), size) for start, size in sizes]
        spans = [
            (0, piece, 0, piece + 1),
            (piece, own_tiles - piece, piece + 1, own_tiles - piece),
            (own_tiles, own_tiles, own_tiles + 1, own_tiles - 1),
        ]
        phases = [(0, side(t, n), n, side(e, m), m) for t, n, e, m in spans]
    else:
        parts = [(0, tiles)]
        phases = []
        for step in range(gz_count):
            chunk = lax.rem(gz + 1 + step, gz_count)
            begin, count = chunk * own_tiles, own_tiles + 2
            phases.append((step, begin, own_tiles, jnp.clip(begin - 1, 0, tiles - count), count))

    def load(part):
        start, size = parts[part]
        return pltpu.make_async_copy(
            x_hbm.at[:, :, cols(start, size)], xin.at[:, :, cols(start + 1, size)], load_sem.at[part]
        )

    for part in range(len(parts)):
        load(part).start()

    barrier = pltpu.get_barrier_semaphore()

    @pl.when(has_up)
    def _():
        pl.semaphore_signal(barrier, inc=1, device_id={"xy": xy - 1}, device_id_type=MESH)

    @pl.when(has_down)
    def _():
        pl.semaphore_signal(barrier, inc=1, device_id={"xy": xy + 1}, device_id_type=MESH)

    for step in range(gz_count - 1):
        peer = lax.rem(gz + 1 + step, gz_count)
        pl.semaphore_signal(barrier, inc=1, device_id={"gz": peer}, device_id_type=MESH)

    def to_up(part):
        start, size = parts[part]
        return pltpu.make_async_remote_copy(
            src_ref=top_out.at[:, cols(start, size)],
            dst_ref=bot_in.at[:, cols(start + 1, size)],
            send_sem=halo_send.at[0, part], recv_sem=halo_recv.at[0, part],
            device_id={"xy": xy - 1}, device_id_type=MESH,
        )

    def to_down(part):
        start, size = parts[part]
        return pltpu.make_async_remote_copy(
            src_ref=bot_out.at[:, cols(start, size)],
            dst_ref=top_in.at[:, cols(start + 1, size)],
            send_sem=halo_send.at[1, part], recv_sem=halo_recv.at[1, part],
            device_id={"xy": xy + 1}, device_id_type=MESH,
        )

    edge = HALO * planes
    for tile in (0, tiles + 1):
        side = pl.ds(tile * LANES, LANES)
        xin[:, :, side] = jnp.zeros((planes, rows, LANES), xin.dtype)
        top_in[:, side] = jnp.zeros((edge, LANES), xin.dtype)
        bot_in[:, side] = jnp.zeros((edge, LANES), xin.dtype)
        vs[:, tile] = jnp.zeros((planes, rows, LANES), jnp.float32)

    inner = pl.ds(LANES, tiles * LANES)

    @pl.when(jnp.logical_not(has_up))
    def _():
        top_in[:, inner] = jnp.zeros((edge, tiles * LANES), xin.dtype)

    @pl.when(jnp.logical_not(has_down))
    def _():
        bot_in[:, inner] = jnp.zeros((edge, tiles * LANES), xin.dtype)

    low = lax.broadcasted_iota(jnp.int32, (8, LANES), 0) < HALO
    for part, (start, size) in enumerate(parts):
        load(part).wait()

        @pl.loop(start, start + size)
        def _(t):
            here = cols(t + 1, 1)
            for p in range(planes):
                xs[t, p, 8 : 8 + rows, :] = xin[p, :, here].astype(jnp.float32)
            out = cols(t, 1)
            for quad in range(planes // 4):
                tops, bots = [], []
                for p in (4 * quad, 4 * quad + 2):
                    tops.append(jnp.where(low, xs[t, p, 8:16, :], xs[t, p + 1, 4:12, :]))
                    bots.append(
                        jnp.where(
                            low,
                            xs[t, p, 4 + rows : 12 + rows, :],
                            xs[t, p + 1, rows : 8 + rows, :],
                        )
                    )
                place = slice(16 * quad, 16 * quad + 16)
                top_out[place, out] = jnp.concatenate(tops, axis=0).astype(xin.dtype)
                bot_out[place, out] = jnp.concatenate(bots, axis=0).astype(xin.dtype)

        if part == 0:
            neighbours = jnp.where(has_up, 1, 0) + jnp.where(has_down, 1, 0) + gz_count - 1
            pl.semaphore_wait(barrier, neighbours)

        @pl.when(has_up)
        def _():
            to_up(part).start()

        @pl.when(has_down)
        def _():
            to_down(part).start()

    source = lax.broadcasted_iota(jnp.int32, (3 * LANES, LANES), 0)
    target = lax.broadcasted_iota(jnp.int32, (3 * LANES, LANES), 1)
    apart = jnp.abs(source - target - LANES)
    centre = jnp.where(apart == 0, 16.0, jnp.where(apart == 1, -2.0, jnp.where(apart == 2, -1.0, 0.0)))
    beside = jnp.where(apart == 0, -2.0, jnp.where(apart == 1, -1.0, 0.0))
    taps[:, 0:LANES] = centre.astype(taps.dtype)
    taps[:, LANES : 2 * LANES] = beside.astype(taps.dtype)

    def own_taps(t):
        wide = xin[:, :, cols(t, 3)].reshape(planes * rows, 3 * LANES)
        both = jnp.dot(wide, taps[...], preferred_element_type=jnp.float32)
        both = both.reshape(planes, rows, 2 * LANES)
        hs[t, :, 8 : 8 + rows, :] = both[:, :, 0:LANES]
        gs[t, :, 8 : 8 + rows, :] = both[:, :, LANES:]

    each(0, tiles, own_taps)

    tall = rows + 8
    lane = lax.broadcasted_iota(jnp.int32, (rows, LANES), 1)
    row_tall = lax.broadcasted_iota(jnp.int32, (tall, LANES), 0)
    first = jnp.where(has_up, 0, 2)
    last = jnp.where(has_down, rows + 4, rows + 2)
    row_mask = jnp.where((row_tall >= first) & (row_tall < last), 1.0, 0.0).astype(jnp.float32)

    def scores(begin, count, e_start, e_count):
        def halo_taps(turn, width):
            first_tile = e_start + turn
            wide = [
                ref[:, cols(first_tile + k, 3)] for k in range(width) for ref in (top_in, bot_in)
            ]
            both = jnp.dot(
                jnp.concatenate(wide, axis=0), taps[...], preferred_element_type=jnp.float32
            )
            for k in range(width):
                t = first_tile + k
                for side, (ref, base) in enumerate(((top_in, 4), (bot_in, 8 + rows))):
                    plain = ref[:, cols(t + 1, 1)].astype(jnp.float32)
                    for p in range(planes):
                        part = slice(HALO * p, HALO * p + HALO)
                        row = (2 * k + side) * edge + HALO * p
                        hs[t, p, base : base + HALO, :] = both[row : row + HALO, 0:LANES]
                        gs[t, p, base : base + HALO, :] = both[row : row + HALO, LANES:]
                        xs[t, p, base : base + HALO, :] = plain[part, :]

        width = e_count if e_count <= 5 else 4

        @pl.loop(0, e_count // width)
        def _(turn):
            halo_taps(turn * width, width)

        if e_count % width:
            halo_taps(e_count - e_count % width, e_count % width)

        @pl.loop(0, planes // 2)
        def _(turn):
            pair_of = [(2 * turn, 0), (2 * turn + 1, 1)]
            for p, bank in pair_of:
                for i in range(e_count):
                    t = e_start + i
                    laplace = (
                        hs[t, p, 6 : 6 + tall, :]
                        + (gs[t, p, 5 : 5 + tall, :] + gs[t, p, 7 : 7 + tall, :])
                        - (xs[t, p, 4 : 4 + tall, :] + xs[t, p, 8 : 8 + tall, :])
                    )
                    es[bank, i, :, :] = laplace * laplace * row_mask
            for p, bank in pair_of:
                for i in range(e_count):
                    column = es[bank, i, 0:rows, :]
                    for k in range(1, 5):
                        column = column + es[bank, i, k : k + rows, :]
                    vs[p, e_start + i + 1] = column
            for p, bank in pair_of:
                flat = [vs[p, begin + i] for i in range(count + 2)]
                right = from_right(flat, 1, lane)
                pair = [flat[i] + right[i] for i in range(count + 1)]
                left = from_left(pair, 2, lane)
                right2 = from_right(flat, 2, lane)
                for i in range(count):
                    ss[p, i] = (pair[i + 1] + left[i] + right2[i + 1]) * sharpness

    def finish(begin, tile, dst):
        peak = ss[0, tile]
        for p in range(1, planes):
            peak = jnp.maximum(peak, ss[p, tile])
        place = begin + tile
        total, blend = None, None
        for p in range(planes):
            weight = jnp.exp(ss[p, tile] - peak)
            term = weight * xs[place, p, 8 : 8 + rows, :]
            total = weight if total is None else total + weight
            blend = term if blend is None else blend + term
        dst[0] = peak + jnp.log(total)
        dst[1] = blend / total

    sends = phases[:-1]

    def to_peer(index):
        step, begin, count, _, _ = sends[index]
        part = pl.ds(lax.rem(begin, own_tiles), count)
        return pltpu.make_async_remote_copy(
            src_ref=outbox.at[step, part], dst_ref=inbox.at[step, part],
            send_sem=gz_send.at[index], recv_sem=gz_recv.at[index],
            device_id={"gz": lax.rem(gz + 1 + step, gz_count)}, device_id_type=MESH,
        )

    def halo_arrived(part):
        @pl.when(has_down)
        def _():
            to_up(part).wait_recv()

        @pl.when(has_up)
        def _():
            to_down(part).wait_recv()

    for index, (step, begin, count, e_start, e_count) in enumerate(phases):
        if index < len(parts):
            halo_arrived(index)
        scores(begin, count, e_start, e_count)
        if index < len(sends):
            inside = lax.rem(begin, own_tiles)
            each(0, count, lambda tile: finish(begin, tile, outbox.at[step, inside + tile]))
            to_peer(index).start()
        else:
            each(0, count, lambda tile: finish(begin, tile, own.at[tile]))

    for index in range(len(sends)):
        to_peer(index).wait()
    for tile in range(own_tiles):
        logs = [own[tile, 0]] + [inbox[s, tile, 0] for s in range(gz_count - 1)]
        means = [own[tile, 1]] + [inbox[s, tile, 1] for s in range(gz_count - 1)]
        peak = functools.reduce(jnp.maximum, logs)
        shares = [jnp.exp(value - peak) for value in logs]
        blend = sum(share * mean for share, mean in zip(shares, means))
        joined = blend / sum(shares)
        joined_ref[:, tile * LANES : (tile + 1) * LANES] = joined
        jt[tile] = joined

    half = rows // 2
    source = lax.broadcasted_iota(jnp.int32, (2 * LANES, LANES), 0)
    target = lax.broadcasted_iota(jnp.int32, (2 * LANES, LANES), 1)
    gather = jnp.where(lax.div(source, 2) == target, 0.25, 0.0).astype(jnp.float32)
    for pair_index in range(own_tiles // 2):
        sides = []
        for tile in (2 * pair_index, 2 * pair_index + 1):
            sides.append(
                jt[tile, pl.ds(0, half, stride=2), :] + jt[tile, pl.ds(1, half, stride=2), :]
            )
        wide = jnp.concatenate(sides, axis=1)
        pooled_ref[:, pair_index * LANES : (pair_index + 1) * LANES] = jnp.dot(
            wide, gather, precision=lax.Precision.HIGHEST, preferred_element_type=jnp.float32
        )

    for part in range(len(parts)):
        @pl.when(has_up)
        def _():
            to_up(part).wait_send()

        @pl.when(has_down)
        def _():
            to_down(part).wait_send()


def shards(gz_count, xy_count, stack):
    planes, rows, breadth = stack.shape
    tiles = breadth // LANES
    own_tiles = tiles // gz_count
    geom = (planes, rows, tiles, gz_count, xy_count, own_tiles)
    f32 = jnp.float32
    padded = breadth + 2 * LANES
    spread = own_tiles + 4
    parts = 3 if gz_count == 2 else 1
    sends = 2 if gz_count == 2 else gz_count - 1
    return pl.pallas_call(
        functools.partial(kernel, geom),
        out_shape=(
            jax.ShapeDtypeStruct((rows, own_tiles * LANES), f32),
            jax.ShapeDtypeStruct((rows // 2, own_tiles * LANES // 2), f32),
        ),
        in_specs=[pl.BlockSpec(memory_space=pltpu.HBM)],
        out_specs=(
            pl.BlockSpec(memory_space=pltpu.VMEM),
            pl.BlockSpec(memory_space=pltpu.VMEM),
        ),
        scratch_shapes=[
            pltpu.VMEM((planes, rows, padded), stack.dtype),
            pltpu.VMEM((planes * HALO, padded), stack.dtype),
            pltpu.VMEM((planes * HALO, padded), stack.dtype),
            pltpu.VMEM((planes * HALO, breadth), stack.dtype),
            pltpu.VMEM((planes * HALO, breadth), stack.dtype),
            pltpu.VMEM((3 * LANES, 2 * LANES), stack.dtype),
            pltpu.VMEM((tiles, planes, rows + 16, LANES), f32),
            pltpu.VMEM((tiles, planes, rows + 16, LANES), f32),
            pltpu.VMEM((tiles, planes, rows + 16, LANES), f32),
            pltpu.VMEM((2, spread, rows + 8, LANES), f32),
            pltpu.VMEM((planes, tiles + 2, rows, LANES), f32),
            pltpu.VMEM((planes, own_tiles, rows, LANES), f32),
            pltpu.VMEM((own_tiles, 2, rows, LANES), f32),
            pltpu.VMEM((gz_count - 1, own_tiles, 2, rows, LANES), f32),
            pltpu.VMEM((gz_count - 1, own_tiles, 2, rows, LANES), f32),
            pltpu.VMEM((own_tiles, rows, LANES), f32),
            pltpu.SemaphoreType.DMA((parts,)),
            pltpu.SemaphoreType.DMA((2, parts)),
            pltpu.SemaphoreType.DMA((2, parts)),
            pltpu.SemaphoreType.DMA((sends,)),
            pltpu.SemaphoreType.DMA((sends,)),
        ],
        compiler_params=pltpu.CompilerParams(collective_id=0, has_side_effects=True, vmem_limit_bytes=VMEM_GRANT),
    )(pltpu.with_memory_space_constraint(stack, pltpu.HBM))


def solution(mesh):
    body = functools.partial(shards, mesh.shape["gz"], mesh.shape["xy"])
    in_specs = (P("gz", "xy", None),)
    out_specs = (P("xy", "gz"), P("xy", "gz"))
    return jax.shard_map(body, mesh=mesh, in_specs=in_specs, out_specs=out_specs, check_vma=False)
```

```python
import functools

import jax
import jax.numpy as jnp
from jax import lax
from jax.experimental import pallas as pl
from jax.experimental.pallas import tpu as pltpu
from jax.sharding import PartitionSpec as P

sharpness = 0.016
LANES = 128
HALO = 4
VMEM_GRANT = 32 * 2**20
MESH = pl.DeviceIdType.MESH


def cols(tile, count):
    return pl.ds(pl.multiple_of(tile * LANES, LANES), count * LANES)


def each(start, count, body, width=2):
    @pl.loop(0, count // width)
    def _(turn):
        for k in range(width):
            body(start + turn * width + k)

    for k in range(count - count % width, count):
        body(start + k)


def from_left(tiles, step, lane):
    rolled = [pltpu.roll(t, step, 1) for t in tiles]
    return [jnp.where(lane < step, rolled[i], rolled[i + 1]) for i in range(len(tiles) - 1)]


def from_right(tiles, step, lane):
    rolled = [pltpu.roll(t, LANES - step, 1) for t in tiles]
    return [
        jnp.where(lane < LANES - step, rolled[i], rolled[i + 1]) for i in range(len(tiles) - 1)
    ]


def kernel(
    geom, x_hbm, joined_ref, pooled_ref,
    xin, top_in, bot_in, top_out, bot_out, taps, xs, gs, hs, es, vs, ss, own, outbox, inbox, jt,
    load_sem, halo_send, halo_recv, gz_send, gz_recv,
):
    planes, rows, tiles, gz_count, xy_count, own_tiles = geom
    gz = lax.axis_index("gz")
    xy = lax.axis_index("xy")
    has_up = xy > 0
    has_down = xy < xy_count - 1

    if gz_count == 2:
        piece = own_tiles // 2
        low_side = gz == 1

        def side(start, count):
            return jnp.where(low_side, start, tiles - start - count)

        sizes = [(0, piece + 2), (piece + 2, own_tiles - piece), (own_tiles + 2, own_tiles - 2)]
        parts = [(side(start, size), size) for start, size in sizes]
        spans = [
            (0, piece, 0, piece + 1),
            (piece, own_tiles - piece, piece + 1, own_tiles - piece),
            (own_tiles, own_tiles, own_tiles + 1, own_tiles - 1),
        ]
        phases = [(0, side(t, n), n, side(e, m), m) for t, n, e, m in spans]
    else:
        parts = [(0, tiles)]
        phases = []
        for step in range(gz_count):
            chunk = lax.rem(gz + 1 + step, gz_count)
            begin, count = chunk * own_tiles, own_tiles + 2
            phases.append((step, begin, own_tiles, jnp.clip(begin - 1, 0, tiles - count), count))

    def load(part):
        start, size = parts[part]
        return pltpu.make_async_copy(
            x_hbm.at[:, :, cols(start, size)], xin.at[:, :, cols(start + 1, size)], load_sem.at[part]
        )

    for part in range(len(parts)):
        load(part).start()

    barrier = pltpu.get_barrier_semaphore()

    @pl.when(has_up)
    def _():
        pl.semaphore_signal(barrier, inc=1, device_id={"xy": xy - 1}, device_id_type=MESH)

    @pl.when(has_down)
    def _():
        pl.semaphore_signal(barrier, inc=1, device_id={"xy": xy + 1}, device_id_type=MESH)

    for step in range(gz_count - 1):
        peer = lax.rem(gz + 1 + step, gz_count)
        pl.semaphore_signal(barrier, inc=1, device_id={"gz": peer}, device_id_type=MESH)

    def to_up(part):
        start, size = parts[part]
        return pltpu.make_async_remote_copy(
            src_ref=top_out.at[:, cols(start, size)],
            dst_ref=bot_in.at[:, cols(start + 1, size)],
            send_sem=halo_send.at[0, part], recv_sem=halo_recv.at[0, part],
            device_id={"xy": xy - 1}, device_id_type=MESH,
        )

    def to_down(part):
        start, size = parts[part]
        return pltpu.make_async_remote_copy(
            src_ref=bot_out.at[:, cols(start, size)],
            dst_ref=top_in.at[:, cols(start + 1, size)],
            send_sem=halo_send.at[1, part], recv_sem=halo_recv.at[1, part],
            device_id={"xy": xy + 1}, device_id_type=MESH,
        )

    edge = HALO * planes
    for tile in (0, tiles + 1):
        side = pl.ds(tile * LANES, LANES)
        xin[:, :, side] = jnp.zeros((planes, rows, LANES), xin.dtype)
        top_in[:, side] = jnp.zeros((edge, LANES), xin.dtype)
        bot_in[:, side] = jnp.zeros((edge, LANES), xin.dtype)
        vs[:, tile] = jnp.zeros((planes, rows, LANES), jnp.float32)

    inner = pl.ds(LANES, tiles * LANES)

    @pl.when(jnp.logical_not(has_up))
    def _():
        top_in[:, inner] = jnp.zeros((edge, tiles * LANES), xin.dtype)

    @pl.when(jnp.logical_not(has_down))
    def _():
        bot_in[:, inner] = jnp.zeros((edge, tiles * LANES), xin.dtype)

    low = lax.broadcasted_iota(jnp.int32, (8, LANES), 0) < HALO
    for part, (start, size) in enumerate(parts):
        load(part).wait()

        @pl.loop(start, start + size)
        def _(t):
            here = cols(t + 1, 1)
            for p in range(planes):
                xs[t, p, 8 : 8 + rows, :] = xin[p, :, here].astype(jnp.float32)
            out = cols(t, 1)
            for quad in range(planes // 4):
                tops, bots = [], []
                for p in (4 * quad, 4 * quad + 2):
                    tops.append(jnp.where(low, xs[t, p, 8:16, :], xs[t, p + 1, 4:12, :]))
                    bots.append(
                        jnp.where(
                            low,
                            xs[t, p, 4 + rows : 12 + rows, :],
                            xs[t, p + 1, rows : 8 + rows, :],
                        )
                    )
                place = slice(16 * quad, 16 * quad + 16)
                top_out[place, out] = jnp.concatenate(tops, axis=0).astype(xin.dtype)
                bot_out[place, out] = jnp.concatenate(bots, axis=0).astype(xin.dtype)

        if part == 0:
            neighbours = jnp.where(has_up, 1, 0) + jnp.where(has_down, 1, 0) + gz_count - 1
            pl.semaphore_wait(barrier, neighbours)

        @pl.when(has_up)
        def _():
            to_up(part).start()

        @pl.when(has_down)
        def _():
            to_down(part).start()

    source = lax.broadcasted_iota(jnp.int32, (3 * LANES, LANES), 0)
    target = lax.broadcasted_iota(jnp.int32, (3 * LANES, LANES), 1)
    apart = jnp.abs(source - target - LANES)
    centre = jnp.where(apart == 0, 16.0, jnp.where(apart == 1, -2.0, jnp.where(apart == 2, -1.0, 0.0)))
    beside = jnp.where(apart == 0, -2.0, jnp.where(apart == 1, -1.0, 0.0))
    taps[:, 0:LANES] = centre.astype(taps.dtype)
    taps[:, LANES : 2 * LANES] = beside.astype(taps.dtype)

    def own_taps(t):
        wide = xin[:, :, cols(t, 3)].reshape(planes * rows, 3 * LANES)
        both = jnp.dot(wide, taps[...], preferred_element_type=jnp.float32)
        both = both.reshape(planes, rows, 2 * LANES)
        hs[t, :, 8 : 8 + rows, :] = both[:, :, 0:LANES]
        gs[t, :, 8 : 8 + rows, :] = both[:, :, LANES:]

    each(0, tiles, own_taps)

    tall = rows + 8
    lane = lax.broadcasted_iota(jnp.int32, (rows, LANES), 1)
    row_tall = lax.broadcasted_iota(jnp.int32, (tall, LANES), 0)
    first = jnp.where(has_up, 0, 2)
    last = jnp.where(has_down, rows + 4, rows + 2)
    row_mask = jnp.where((row_tall >= first) & (row_tall < last), 1.0, 0.0).astype(jnp.float32)

    def scores(begin, count, e_start, e_count):
        def halo_taps(turn, width):
            first_tile = e_start + turn
            wide = [
                ref[:, cols(first_tile + k, 3)] for k in range(width) for ref in (top_in, bot_in)
            ]
            both = jnp.dot(
                jnp.concatenate(wide, axis=0), taps[...], preferred_element_type=jnp.float32
            )
            for k in range(width):
                t = first_tile + k
                for side, (ref, base) in enumerate(((top_in, 4), (bot_in, 8 + rows))):
                    plain = ref[:, cols(t + 1, 1)].astype(jnp.float32)
                    for p in range(planes):
                        part = slice(HALO * p, HALO * p + HALO)
                        row = (2 * k + side) * edge + HALO * p
                        hs[t, p, base : base + HALO, :] = both[row : row + HALO, 0:LANES]
                        gs[t, p, base : base + HALO, :] = both[row : row + HALO, LANES:]
                        xs[t, p, base : base + HALO, :] = plain[part, :]

        width = e_count if e_count <= 5 else 4

        @pl.loop(0, e_count // width)
        def _(turn):
            halo_taps(turn * width, width)

        if e_count % width:
            halo_taps(e_count - e_count % width, e_count % width)

        @pl.loop(0, planes // 2)
        def _(turn):
            pair_of = [(2 * turn, 0), (2 * turn + 1, 1)]
            for p, bank in pair_of:
                for i in range(e_count):
                    t = e_start + i
                    laplace = (
                        hs[t, p, 6 : 6 + tall, :]
                        + (gs[t, p, 5 : 5 + tall, :] + gs[t, p, 7 : 7 + tall, :])
                        - (xs[t, p, 4 : 4 + tall, :] + xs[t, p, 8 : 8 + tall, :])
                    )
                    es[bank, i, :, :] = laplace * laplace * row_mask
            for p, bank in pair_of:
                for i in range(e_count):
                    column = es[bank, i, 0:rows, :]
                    for k in range(1, 5):
                        column = column + es[bank, i, k : k + rows, :]
                    vs[p, e_start + i + 1] = column
            for p, bank in pair_of:
                flat = [vs[p, begin + i] for i in range(count + 2)]
                right = from_right(flat, 1, lane)
                pair = [flat[i] + right[i] for i in range(count + 1)]
                left = from_left(pair, 2, lane)
                right2 = from_right(flat, 2, lane)
                for i in range(count):
                    ss[p, i] = (pair[i + 1] + left[i] + right2[i + 1]) * sharpness

    def finish(begin, tile, dst):
        peak = ss[0, tile]
        for p in range(1, planes):
            peak = jnp.maximum(peak, ss[p, tile])
        place = begin + tile
        total, blend = None, None
        for p in range(planes):
            weight = jnp.exp(ss[p, tile] - peak)
            term = weight * xs[place, p, 8 : 8 + rows, :]
            total = weight if total is None else total + weight
            blend = term if blend is None else blend + term
        dst[0] = peak + jnp.log(total)
        dst[1] = blend / total

    sends = phases[:-1]

    def to_peer(index):
        step, begin, count, _, _ = sends[index]
        part = pl.ds(lax.rem(begin, own_tiles), count)
        return pltpu.make_async_remote_copy(
            src_ref=outbox.at[step, part], dst_ref=inbox.at[step, part],
            send_sem=gz_send.at[index], recv_sem=gz_recv.at[index],
            device_id={"gz": lax.rem(gz + 1 + step, gz_count)}, device_id_type=MESH,
        )

    def halo_arrived(part):
        @pl.when(has_down)
        def _():
            to_up(part).wait_recv()

        @pl.when(has_up)
        def _():
            to_down(part).wait_recv()

    for index, (step, begin, count, e_start, e_count) in enumerate(phases):
        if index < len(parts):
            halo_arrived(index)
        scores(begin, count, e_start, e_count)
        if index < len(sends):
            inside = lax.rem(begin, own_tiles)
            each(0, count, lambda tile: finish(begin, tile, outbox.at[step, inside + tile]))
            to_peer(index).start()
        else:
            each(0, count, lambda tile: finish(begin, tile, own.at[tile]))

    for index in range(len(sends)):
        to_peer(index).wait()
    for tile in range(own_tiles):
        logs = [own[tile, 0]] + [inbox[s, tile, 0] for s in range(gz_count - 1)]
        means = [own[tile, 1]] + [inbox[s, tile, 1] for s in range(gz_count - 1)]
        peak = functools.reduce(jnp.maximum, logs)
        shares = [jnp.exp(value - peak) for value in logs]
        blend = sum(share * mean for share, mean in zip(shares, means))
        joined = blend / sum(shares)
        joined_ref[:, tile * LANES : (tile + 1) * LANES] = joined
        jt[tile] = joined

    half = rows // 2
    source = lax.broadcasted_iota(jnp.int32, (2 * LANES, LANES), 0)
    target = lax.broadcasted_iota(jnp.int32, (2 * LANES, LANES), 1)
    gather = jnp.where(lax.div(source, 2) == target, 0.25, 0.0).astype(jnp.float32)
    for pair_index in range(own_tiles // 2):
        sides = []
        for tile in (2 * pair_index, 2 * pair_index + 1):
            sides.append(
                jt[tile, pl.ds(0, half, stride=2), :] + jt[tile, pl.ds(1, half, stride=2), :]
            )
        wide = jnp.concatenate(sides, axis=1)
        pooled_ref[:, pair_index * LANES : (pair_index + 1) * LANES] = jnp.dot(
            wide, gather, precision=lax.Precision.HIGHEST, preferred_element_type=jnp.float32
        )

    for part in range(len(parts)):
        @pl.when(has_up)
        def _():
            to_up(part).wait_send()

        @pl.when(has_down)
        def _():
            to_down(part).wait_send()


def write_out(joined_in, pooled_in, joined_out, pooled_out, sems):
    copies = [
        pltpu.make_async_copy(joined_in, joined_out, sems.at[0]),
        pltpu.make_async_copy(pooled_in, pooled_out, sems.at[1]),
    ]
    for copy in copies:
        copy.start()
    for copy in copies:
        copy.wait()


def shards(gz_count, xy_count, stack):
    planes, rows, breadth = stack.shape
    tiles = breadth // LANES
    own_tiles = tiles // gz_count
    geom = (planes, rows, tiles, gz_count, xy_count, own_tiles)
    f32 = jnp.float32
    padded = breadth + 2 * LANES
    spread = own_tiles + 4
    parts = 3 if gz_count == 2 else 1
    sends = 2 if gz_count == 2 else gz_count - 1
    joined, pooled = pl.pallas_call(
        functools.partial(kernel, geom),
        out_shape=(
            jax.ShapeDtypeStruct((rows, own_tiles * LANES), f32),
            jax.ShapeDtypeStruct((rows // 2, own_tiles * LANES // 2), f32),
        ),
        in_specs=[pl.BlockSpec(memory_space=pltpu.HBM)],
        out_specs=(
            pl.BlockSpec(memory_space=pltpu.VMEM),
            pl.BlockSpec(memory_space=pltpu.VMEM),
        ),
        scratch_shapes=[
            pltpu.VMEM((planes, rows, padded), stack.dtype),
            pltpu.VMEM((planes * HALO, padded), stack.dtype),
            pltpu.VMEM((planes * HALO, padded), stack.dtype),
            pltpu.VMEM((planes * HALO, breadth), stack.dtype),
            pltpu.VMEM((planes * HALO, breadth), stack.dtype),
            pltpu.VMEM((3 * LANES, 2 * LANES), stack.dtype),
            pltpu.VMEM((tiles, planes, rows + 16, LANES), f32),
            pltpu.VMEM((tiles, planes, rows + 16, LANES), f32),
            pltpu.VMEM((tiles, planes, rows + 16, LANES), f32),
            pltpu.VMEM((2, spread, rows + 8, LANES), f32),
            pltpu.VMEM((planes, tiles + 2, rows, LANES), f32),
            pltpu.VMEM((planes, own_tiles, rows, LANES), f32),
            pltpu.VMEM((own_tiles, 2, rows, LANES), f32),
            pltpu.VMEM((gz_count - 1, own_tiles, 2, rows, LANES), f32),
            pltpu.VMEM((gz_count - 1, own_tiles, 2, rows, LANES), f32),
            pltpu.VMEM((own_tiles, rows, LANES), f32),
            pltpu.SemaphoreType.DMA((parts,)),
            pltpu.SemaphoreType.DMA((2, parts)),
            pltpu.SemaphoreType.DMA((2, parts)),
            pltpu.SemaphoreType.DMA((sends,)),
            pltpu.SemaphoreType.DMA((sends,)),
        ],
        compiler_params=pltpu.CompilerParams(collective_id=0, has_side_effects=True, vmem_limit_bytes=VMEM_GRANT),
    )(pltpu.with_memory_space_constraint(stack, pltpu.HBM))
    return pl.pallas_call(
        write_out,
        out_shape=(
            jax.ShapeDtypeStruct(joined.shape, f32),
            jax.ShapeDtypeStruct(pooled.shape, f32),
        ),
        in_specs=[pl.BlockSpec(memory_space=pltpu.VMEM)] * 2,
        out_specs=(
            pl.BlockSpec(memory_space=pltpu.HBM),
            pl.BlockSpec(memory_space=pltpu.HBM),
        ),
        scratch_shapes=[pltpu.SemaphoreType.DMA((2,))],
        compiler_params=pltpu.CompilerParams(vmem_limit_bytes=2**20),
    )(joined, pooled)


def solution(mesh):
    body = functools.partial(shards, mesh.shape["gz"], mesh.shape["xy"])
    in_specs = (P("gz", "xy", None),)
    out_specs = (P("xy", "gz"), P("xy", "gz"))
    return jax.shard_map(body, mesh=mesh, in_specs=in_specs, out_specs=out_specs, check_vma=False)
```
